32 devices in a mesh: row: 8 (over z, y), col: 4 (over x, core).
Axes of the slice: x: 2, y: 2, z: 4, core: 2. Of those that a mesh axis runs over, the one named last changes fastest.
Arguments:
- inputs: bfloat16 [128, 8192], P('row', 'col'), may hold values from -6 to 6
- out_grad: bfloat16 [128, 8192], P('row', 'col'), may hold values from -96 to 96
- gate_weight: bfloat16 [8192, 16384], P('col', 'row'), may hold values from -0.0625 to 0.0625
- up_weight: bfloat16 [8192, 16384], P('col', 'row'), may hold values from -0.0625 to 0.0625
- down_weight: bfloat16 [16384, 8192], P('row', 'col'), may hold values from -0.046875 to 0.046875
Outputs:
- input_grad: bfloat16 [128, 8192], P('row', 'col')
- gate_grad: bfloat16 [8192, 16384], P('col', 'row')
- up_grad: bfloat16 [8192, 16384], P('col', 'row')
- down_grad: bfloat16 [16384, 8192], P('row', 'col')
The draws below stay inside these ranges and needn't reach their ends.
All inputs are finite; a program needn't handle non-finite values.
Results may differ from the reference program's by a relative error of at most 0.005.
Values may be sent and summed in bfloat16 or wider, within the bound.
No kernel may reach another device: no remote copies, remote signals or barrier semaphores. Data moves between devices by JAX's collectives and lax.ppermute only.
A program may use at most 128 MiB of HBM per device.

```python
import jax
import jax.numpy as jnp
from jax import lax

D = 8192
FF = 16384
LAYERS = 128
TOKENS = 128


def levels(own_key, dims, shards, low, high):
    factor_of = 1.0
    for axis_at, shards_of in shards:
        steps = jax.random.uniform(jax.random.fold_in(jax.random.fold_in(own_key, 6), axis_at), (shards_of,), jnp.float32, low / len(shards), high / len(shards))
        factor_of = factor_of * jnp.repeat(jnp.exp(steps), dims[axis_at] // shards_of).reshape((-1,) + (1,) * (len(dims) - 1 - axis_at))
    return factor_of


def scatter_about(own_key, shape, deviation, bound, shards=(), kind=jnp.bfloat16):
    drawn = jax.random.normal(own_key, shape, jnp.float32) * deviation
    if len(shards) > 0:
        drawn = levels(own_key, shape, shards, -0.22, 0.18) * drawn
    return jnp.clip(drawn, min=-bound, max=bound).astype(kind)


def setup_inputs(seed: int = 0) -> dict:
    splits = jax.random.split(jax.random.key(seed), 6)
    return {
        "inputs": scatter_about(splits[0], (TOKENS, D), 1.0, 6.0, ((0, 8), (1, 4))),
        "out_grad": scatter_about(splits[1], (TOKENS, D), 16.0, 96.0, ((0, 8), (1, 4))),
        "gate_weight": scatter_about(splits[2], (D, FF), D ** -0.5, 0.0625, ((0, 4), (1, 8))),
        "up_weight": scatter_about(splits[3], (D, FF), D ** -0.5, 0.0625, ((0, 4), (1, 8))),
        "down_weight": scatter_about(splits[4], (FF, D), FF ** -0.5, 0.046875, ((0, 8), (1, 4))),
    }


def reference(inputs, out_grad, gate_weight, up_weight, down_weight):
    mult = (2.0 * LAYERS) ** -0.5
    gate = jnp.dot(inputs, gate_weight, preferred_element_type=jnp.float32)
    up = jnp.dot(inputs, up_weight, preferred_element_type=jnp.float32)
    sig = jax.nn.sigmoid(gate)
    hidden = (gate * sig * up).astype(jnp.bfloat16)
    back = lax.dot_general(out_grad, down_weight, (((1,), (1,)), ((), ())), preferred_element_type=jnp.float32)
    hidden_grad = mult * back
    gate_delta = (hidden_grad * up * sig * (1.0 + gate * (1.0 - sig))).astype(jnp.bfloat16)
    up_delta = (hidden_grad * gate * sig).astype(jnp.bfloat16)
    down_grad = (mult * lax.dot_general(hidden, out_grad, (((0,), (0,)), ((), ())), preferred_element_type=jnp.float32)).astype(jnp.bfloat16)
    gate_grad = lax.dot_general(inputs, gate_delta, (((0,), (0,)), ((), ())), preferred_element_type=jnp.float32).astype(jnp.bfloat16)
    up_grad = lax.dot_general(inputs, up_delta, (((0,), (0,)), ((), ())), preferred_element_type=jnp.float32).astype(jnp.bfloat16)
    input_grad = lax.dot_general(gate_delta, gate_weight, (((1,), (1,)), ((), ())), preferred_element_type=jnp.float32)
    input_grad = input_grad + lax.dot_general(up_delta, up_weight, (((1,), (1,)), ((), ())), preferred_element_type=jnp.float32)
    return input_grad.astype(jnp.bfloat16), gate_grad, up_grad, down_grad
```

```python
import functools

import jax
import jax.numpy as jnp
from jax import lax
from jax.experimental import pallas as pl
from jax.experimental.pallas import tpu as pltpu
from jax.sharding import PartitionSpec as P

LAYERS = 128
F32 = jnp.float32
BF16 = jnp.bfloat16


def contract_rows(left, right):
    return lax.dot_general(left, right, (((0,), (0,)), ((), ())), preferred_element_type=F32)


def contract_cols(left, right):
    return lax.dot_general(left, right, (((1,), (1,)), ((), ())), preferred_element_type=F32)


def swap(value, axis, size, bit):
    return lax.ppermute(value, axis, [(i, i ^ (1 << bit)) for i in range(size)])


def bits_of(size):
    return size.bit_length() - 1


def outer_kernel(scale, rows, left_ref, right_ref, out_ref, held, sems):
    total = out_ref.shape[0]
    slots = held.shape[0]
    copies = []
    for step in range(total // rows):
        slot = step % slots
        if step >= slots:
            copies[step - slots].wait()
        value = contract_rows(left_ref[:, pl.ds(step * rows, rows)], right_ref[...])
        if scale is not None:
            value = scale * value
        held[slot] = value.astype(held.dtype)
        copy = pltpu.make_async_copy(held.at[slot], out_ref.at[pl.ds(step * rows, rows)], sems.at[slot])
        copy.start()
        copies.append(copy)
    for copy in copies[-slots:]:
        copy.wait()


def outer(left, right, scale=None):
    tokens, height = left.shape
    width = right.shape[1]
    rows, slots = min(256, height), 4
    return pl.pallas_call(
        functools.partial(outer_kernel, scale, rows),
        out_shape=jax.ShapeDtypeStruct((height, width), BF16),
        in_specs=[pl.BlockSpec(memory_space=pltpu.VMEM)] * 2,
        out_specs=pl.BlockSpec(memory_space=pl.ANY),
        scratch_shapes=[pltpu.VMEM((slots, rows, width), BF16), pltpu.SemaphoreType.DMA((slots,))],
        cost_estimate=pl.CostEstimate(
            flops=2 * tokens * height * width,
            bytes_accessed=2 * (height * width + tokens * (height + width)),
            transcendentals=0,
        ),
        compiler_params=pltpu.CompilerParams(vmem_limit_bytes=24 << 20),
    )(left, right)


def gather(value, axis, size, order):
    offsets = [0]
    for bit in order:
        value = jnp.concatenate([value, swap(value, axis, size, bit)])
        offsets += [offset ^ (1 << bit) for offset in offsets]
    return value, offsets


def reorder(value, held, wanted):
    if held == wanted:
        return value
    block = value.shape[0] // len(held)
    return jnp.concatenate([value[held.index(o) * block : (held.index(o) + 1) * block] for o in wanted])


def scatter(value, axis, size, order):
    for bit in reversed(order):
        half = value.shape[0] // 2
        value = value[:half] + swap(value[half:].astype(BF16), axis, size, bit).astype(F32)
    return value


def halve(value, axis, size, bit):
    half = value.shape[-2] // 2
    upper = (lax.axis_index(axis) >> bit) & 1
    mine = lax.dynamic_slice_in_dim(value, upper * half, half, value.ndim - 2)
    other = lax.dynamic_slice_in_dim(value, (1 - upper) * half, half, value.ndim - 2)
    return mine + swap(other, axis, size, bit)


def double(value, axis, size, bit):
    upper = (lax.axis_index(axis) >> bit) & 1
    other = swap(value, axis, size, bit)
    return jnp.where(upper == 0, jnp.concatenate([value, other], -2), jnp.concatenate([other, value], -2))


def reduce_part(value, size):
    high = bits_of(size) - 1
    for bit in range(high):
        value = halve(value, "col", size, bit)
    if high >= 0:
        value = value + swap(value.astype(BF16), "col", size, high).astype(F32)
    return value


def per_device(sizes, inputs, out_grad, gate_weight, up_weight, down_weight):
    mult = (2.0 * LAYERS) ** (-0.5)
    rows, cols = sizes
    bits = list(range(bits_of(rows)))
    order = bits[::-1]
    other_order = order
    tokens_all, offsets = gather(inputs, "row", rows, order)
    grads_all, held = gather(out_grad, "row", rows, other_order)
    grads_all = reorder(grads_all, held, offsets)

    gate = reduce_part(jnp.dot(tokens_all, gate_weight, preferred_element_type=F32), cols)
    up = reduce_part(jnp.dot(tokens_all, up_weight, preferred_element_type=F32), cols)
    back = reduce_part(contract_cols(grads_all, down_weight), cols)

    sig = jax.nn.sigmoid(gate)
    hidden_grad = mult * back
    hidden = (gate * sig * up).astype(BF16)
    gate_delta = (hidden_grad * up * sig * (1.0 + gate * (1.0 - sig))).astype(BF16)
    up_delta = (hidden_grad * gate * sig).astype(BF16)
    deltas = jnp.stack([gate_delta, up_delta])
    for bit in reversed(range(bits_of(cols) - 1)):
        hidden = double(hidden, "col", cols, bit)
        deltas = double(deltas, "col", cols, bit)
    gate_delta, up_delta = deltas[0], deltas[1]

    down_grad = outer(hidden, grads_all, mult)
    input_part = contract_cols(gate_delta, gate_weight) + contract_cols(up_delta, up_weight)
    input_grad = scatter(input_part, "row", rows, order).astype(BF16)
    gate_grad = outer(tokens_all, gate_delta)
    up_grad = outer(tokens_all, up_delta)
    return (input_grad, gate_grad, up_grad, down_grad)


def solution(mesh):
    sizes = (mesh.shape["row"], mesh.shape["col"])
    return jax.shard_map(
        functools.partial(per_device, sizes),
        mesh=mesh,
        in_specs=(
            P("row", "col"),
            P("row", "col"),
            P("col", "row"),
            P("col", "row"),
            P("row", "col"),
        ),
        out_specs=(P("row", "col"), P("col", "row"), P("col", "row"), P("row", "col")),
        check_vma=False,
    )
```

```python
import functools

import jax
import jax.numpy as jnp
from jax import lax
from jax.experimental import pallas as pl
from jax.experimental.pallas import tpu as pltpu
from jax.sharding import PartitionSpec as P


LAYERS = 128
F32 = jnp.float32
BF16 = jnp.bfloat16
VMEM = pl.BlockSpec(memory_space=pltpu.VMEM)
SMEM = pl.BlockSpec(memory_space=pltpu.SMEM)
ANY = pl.BlockSpec(memory_space=pl.ANY)
HBM = pl.BlockSpec(memory_space=pltpu.HBM)
LOAD_LIMIT = 44 << 20


def contract_rows(left, right):
    return lax.dot_general(left, right, (((0,), (0,)), ((), ())), preferred_element_type=F32)


def contract_cols(left, right):
    return lax.dot_general(left, right, (((1,), (1,)), ((), ())), preferred_element_type=F32)


def swap(value, axis, size, mask):
    return lax.ppermute(value, axis, [(i, i ^ mask) for i in range(size)])


def bits_of(size):
    return size.bit_length() - 1


def tiles(total, most):
    size = min(total, most)
    return [pl.ds(start, size) for start in range(0, total, size)]


def cost(flops, arrays):
    moved = sum(a.size * a.dtype.itemsize for a in arrays)
    return pl.CostEstimate(flops=flops, bytes_accessed=moved, transcendentals=0)


def into_kernel(half_ref, tokens_ref, weight_ref, own_ref, other_ref):
    width = own_ref.shape[1]
    for out_ref, half in ((other_ref, 1 - half_ref[0]), (own_ref, half_ref[0])):
        start = pl.multiple_of(half * width, width)
        out_ref[...] = jnp.dot(
            tokens_ref[...], weight_ref[:, pl.ds(start, width)], preferred_element_type=F32
        )


def halves(half_ref, tokens_ref, top_ref, bottom_ref, out_ref):
    width, middle = out_ref.shape[1], top_ref.shape[0]
    columns = pl.ds(pl.multiple_of(half_ref[0] * width, width), width)
    value = jnp.dot(tokens_ref[:, :middle], top_ref[:, columns], preferred_element_type=F32)
    value += jnp.dot(tokens_ref[:, middle:], bottom_ref[:, columns], preferred_element_type=F32)
    out_ref[...] = value


def first_kernel(half_ref, *refs):
    *block_refs, top_ref, bottom_ref, out_ref, tokens_ref = refs
    tokens_ref[...] = jnp.concatenate([ref[...] for ref in block_refs])
    halves(half_ref, tokens_ref, top_ref, bottom_ref, out_ref)


def load_kernel(starts, *refs):
    count = len(starts)
    copies = []
    for k, (start, ref, out_ref) in enumerate(zip(starts, refs, refs[count:])):
        source = ref.at[pl.ds(start, out_ref.shape[0])]
        copies.append(pltpu.make_async_copy(source, out_ref, refs[-1].at[k]))
    for copy in copies:
        copy.start()
    for copy in copies:
        copy.wait()


def load(limit, *spans):
    count = len(spans)
    shapes = tuple(jax.ShapeDtypeStruct((rows, a.shape[1]), a.dtype) for a, _, rows in spans)
    total = sum(shape.size * shape.dtype.itemsize for shape in shapes)
    return pl.pallas_call(
        functools.partial(load_kernel, [start for _, start, _ in spans]),
        out_shape=shapes,
        in_specs=[HBM] * count,
        out_specs=(VMEM,) * count,
        scratch_shapes=[pltpu.SemaphoreType.DMA((count,))],
        cost_estimate=cost(0, shapes),
        compiler_params=pltpu.CompilerParams(vmem_limit_bytes=limit),
    )(*[a for a, _, _ in spans])


def into_half(kernel, half, blocks, *weights):
    count = sum(block.shape[0] for block in blocks)
    shape = jax.ShapeDtypeStruct((count, weights[0].shape[1] // 2), F32)
    tokens = jax.ShapeDtypeStruct((count, blocks[0].shape[1]), BF16)
    shapes = (shape, tokens) if len(blocks) > 1 else (shape,)
    return pl.pallas_call(
        kernel,
        out_shape=shapes,
        in_specs=[SMEM] + [VMEM] * (len(blocks) + 2),
        out_specs=(VMEM,) * len(shapes),
        cost_estimate=cost(2 * count * weights[0].size, [*blocks, *weights, *shapes]),
        compiler_params=pltpu.CompilerParams(vmem_limit_bytes=12 << 20),
    )(half, *blocks, *weights)


def back_kernel(half_ref, tokens_ref, weight_ref, turn_ref, own_ref, other_ref, turned_ref):
    turned_ref[...] = turn_ref[...].T
    width = own_ref.shape[1]
    step = min(width, 512)
    for out_ref, half in ((other_ref, 1 - half_ref[0]), (own_ref, half_ref[0])):
        for at in range(0, width, step):
            start = pl.multiple_of(half * width + at, step)
            value = contract_cols(weight_ref[pl.ds(start, step), :], tokens_ref[...])
            out_ref[:, pl.ds(at, step)] = value.T


def into_hidden(kernel, half, tokens, weight, hidden, *turn):
    shape = jax.ShapeDtypeStruct((tokens.shape[0], hidden // 2), F32)
    turned = [jax.ShapeDtypeStruct(a.shape[::-1], a.dtype) for a in turn]
    return pl.pallas_call(
        kernel,
        out_shape=(shape, shape, *turned),
        in_specs=[SMEM, VMEM, VMEM] + [VMEM] * len(turn),
        out_specs=(VMEM, VMEM) + (VMEM,) * len(turn),
        cost_estimate=cost(2 * tokens.shape[0] * weight.size, [tokens, weight, shape, shape]),
        compiler_params=pltpu.CompilerParams(vmem_limit_bytes=12 << 20),
    )(half, tokens, weight, *turn)


def out_kernel(half_ref, gate_ref, up_ref, top_ref, bottom_ref, up_weight_ref, *rest):
    out_ref = rest[-1]
    width, middle = gate_ref.shape[1], top_ref.shape[0]
    columns = pl.ds(pl.multiple_of(half_ref[0] * width, width), width)
    for part, ref in enumerate((top_ref, bottom_ref)):
        for rows in tiles(middle, 512):
            into = pl.ds(part * middle + rows.start, rows.size)
            value = contract_cols(ref[rows, columns], gate_ref[...])
            value += contract_cols(up_weight_ref[into, columns], up_ref[...])
            value = value.T
            if len(rest) > 1:
                value += rest[0][:, into]
            out_ref[:, into] = value


def out_of_hidden(half, gate, up, top, bottom, up_weight, *total):
    shape = jax.ShapeDtypeStruct((gate.shape[0], up_weight.shape[0]), F32)
    arrays = [gate, up, top, bottom, up_weight, *total]
    return pl.pallas_call(
        out_kernel,
        out_shape=shape,
        in_specs=[SMEM] + [VMEM] * len(arrays),
        out_specs=VMEM,
        cost_estimate=cost(4 * gate.size * up_weight.shape[0], arrays + [shape]),
        compiler_params=pltpu.CompilerParams(vmem_limit_bytes=21 << 20),
    )(half, *arrays)


def write_out(slices, held, sems):
    slots = held.shape[0]
    copies = []
    for step, (make, target) in enumerate(slices):
        slot = step % slots
        if step >= slots:
            copies[step - slots].wait()
        value = make().astype(held.dtype)
        held[slot] = value
        copy = pltpu.make_async_copy(held.at[slot], target, sems.at[slot])
        copy.start()
        copies.append(copy)
    for copy in copies[-slots:]:
        copy.wait()


def down_kernel(scale, half_ref, own_ref, other_ref, grads_ref, out_ref, held, sems):
    rows = held.shape[1]
    width = own_ref.shape[1]
    slices = []
    for ref, half in ((own_ref, half_ref[0]), (other_ref, 1 - half_ref[0])):
        for at in range(0, width, rows):
            make = lambda ref=ref, at=at: scale * contract_rows(ref[:, pl.ds(at, rows)], grads_ref[...])
            start = pl.multiple_of(half * width + at, rows)
            slices.append((make, out_ref.at[pl.ds(start, rows)]))
    write_out(slices, held, sems)


def down_outer(scale, half, own, other, grads):
    tokens, width = own.shape
    features = grads.shape[1]
    rows, slots = min(256, width), 4
    shape = jax.ShapeDtypeStruct((2 * width, features), BF16)
    return pl.pallas_call(
        functools.partial(down_kernel, scale),
        out_shape=shape,
        in_specs=[SMEM, VMEM, VMEM, VMEM],
        out_specs=ANY,
        scratch_shapes=[pltpu.VMEM((slots, rows, features), BF16), pltpu.SemaphoreType.DMA((slots,))],
        cost_estimate=cost(4 * tokens * width * features, [own, other, grads, shape]),
        compiler_params=pltpu.CompilerParams(vmem_limit_bytes=10 << 20),
    )(half, own, other, grads)


def up_kernel(units, count, half_ref, turned_ref, *refs):
    part_refs = refs[: len(units)]
    out_refs, held, sems = refs[-2 - count : -2], refs[-2], refs[-1]
    rows, width = held.shape[1:]
    slices = []
    for (out, own), ref in zip(units, part_refs):
        half = half_ref[0] if own else 1 - half_ref[0]
        columns = pl.ds(pl.multiple_of(half * width, width), width)
        for at in range(0, turned_ref.shape[0], rows):
            make = lambda ref=ref, at=at: jnp.dot(
                turned_ref[pl.ds(at, rows), :], ref[...], preferred_element_type=F32
            )
            slices.append((make, out_refs[out].at[pl.ds(at, rows), columns]))
    write_out(slices, held, sems)


def up_outer(half, turned, parts, begun=None, fresh=0):
    features, _ = turned.shape
    width = parts[0][2].shape[1]
    rows, slots = min(512, features), 4
    shape = jax.ShapeDtypeStruct((features, 2 * width), BF16)
    deltas = [part[2] for part in parts]
    kept = [] if begun is None else [begun]
    outs = len(kept) + fresh
    return pl.pallas_call(
        functools.partial(up_kernel, [part[:2] for part in parts], outs),
        out_shape=(shape,) * outs,
        in_specs=[SMEM] + [VMEM] * (1 + len(deltas)) + [ANY] * len(kept),
        out_specs=(ANY,) * outs,
        scratch_shapes=[pltpu.VMEM((slots, rows, width), BF16), pltpu.SemaphoreType.DMA((slots,))],
        input_output_aliases={2 + len(deltas): 0} if kept else {},
        cost_estimate=cost(2 * turned.size * width * len(deltas), [turned, *deltas, *deltas]),
        compiler_params=pltpu.CompilerParams(vmem_limit_bytes=10 << 20),
    )(half, turned, *deltas, *kept)


def gather(value, near, size, separate):
    for bit in range(3, bits_of(size)):
        value = near = jnp.concatenate([near, swap(value, "row", size, 1 << bit)])
    far = [swap(value, "row", size, 4)]
    if not separate:
        blocks = jnp.concatenate([near] + far)
        blocks = jnp.concatenate([blocks, swap(blocks, "row", size, 2)])
        return [blocks, swap(blocks, "row", size, 1)]
    far += [swap(value, "row", size, 2)]
    near_1 = swap(value, "row", size, 1)
    far += [swap(far[0], "row", size, 2)]
    near_53 = swap(jnp.concatenate(far[:2]), "row", size, 1)
    return [near, *far, near_1, near_53, swap(far[2], "row", size, 1)]


def scatter(value, size):
    def add(kept, sent, mask):
        return kept + swap(sent.astype(BF16), "row", size, mask).astype(F32)

    count = value.shape[0] // 4
    kept, last, sent_kept, sent_last = (value[k * count : (k + 1) * count] for k in range(4))
    last = add(last, sent_last, 1)
    kept = add(kept, sent_kept, 1)
    value = add(kept, last, 2)
    for bit in [2] + list(range(3, bits_of(size)))[::-1]:
        half = value.shape[0] // 2
        value = add(value[:half], value[half:], 1 << bit)
    return value


def feature_sum(parts, size):
    own, other = parts
    total = own + swap(other, "col", size, 1)
    for bit in range(1, bits_of(size)):
        sent = total.astype(BF16)
        total = total + swap(sent, "col", size, 1 << bit).astype(F32)
    return total


def per_device(sizes, inputs, out_grad, gate_weight, up_weight, down_weight):
    mult = (2.0 * LAYERS) ** (-0.5)
    rows, cols = sizes
    hidden_units = gate_weight.shape[1]
    half = (lax.axis_index("col") & 1).astype(jnp.int32).reshape(1)
    own, own_grad = load(1 << 20, (inputs, 0, inputs.shape[0]), (out_grad, 0, out_grad.shape[0]))
    blocks = gather(inputs, own, rows, True)
    grads_all = jnp.concatenate(gather(out_grad, own_grad, rows, False))
    middle = gate_weight.shape[0] // 2
    (gate_top,) = load(LOAD_LIMIT, (gate_weight, 0, middle))
    (gate_bottom,) = load(LOAD_LIMIT, (gate_weight, middle, middle))
    other, tokens_all = into_half(first_kernel, 1 - half, blocks, gate_top, gate_bottom)
    parts = [*into_half(halves, half, [tokens_all], gate_top, gate_bottom), other]
    gate = feature_sum(parts, cols)
    parts = into_hidden(into_kernel, half, tokens_all, up_weight, hidden_units)
    up = feature_sum(parts, cols)
    *parts, tokens_turned = into_hidden(back_kernel, half, grads_all, down_weight, hidden_units, tokens_all)
    back = feature_sum(parts, cols)

    hidden = (gate * jax.nn.sigmoid(gate) * up).astype(BF16)
    hidden_other = swap(hidden, "col", cols, 1)
    down_grad = down_outer(mult, half, hidden, hidden_other, grads_all)

    gate, up, back = lax.optimization_barrier((gate, up, back))
    sig = jax.nn.sigmoid(gate)
    hidden_grad = mult * back
    gate_delta = (hidden_grad * up * sig * (1.0 + gate * (1.0 - sig))).astype(BF16)
    up_delta = (hidden_grad * gate * sig).astype(BF16)
    gate_other = swap(gate_delta, "col", cols, 1)
    up_other = swap(up_delta, "col", cols, 1)

    part = out_of_hidden(half, gate_delta, up_delta, gate_top, gate_bottom, up_weight)
    part = out_of_hidden(1 - half, gate_other, up_other, gate_top, gate_bottom, up_weight, part)
    input_grad = scatter(part, rows).astype(BF16)
    (gate_grad,) = up_outer(half, tokens_turned, [(0, True, gate_delta)], fresh=1)
    parts = [(0, False, gate_other), (1, True, up_delta)]
    gate_grad, up_grad = up_outer(half, tokens_turned, parts, gate_grad, fresh=1)
    (up_grad,) = up_outer(half, tokens_turned, [(0, False, up_other)], up_grad)
    return (input_grad, gate_grad, up_grad, down_grad)


def whole(sizes, *arrays):
    return per_device(sizes, *arrays)


def solution(mesh):
    sizes = (mesh.shape["row"], mesh.shape["col"])
    return jax.shard_map(
        functools.partial(whole, sizes),
        mesh=mesh,
        in_specs=(
            P("row", "col"),
            P("row", "col"),
            P("col", "row"),
            P("col", "row"),
            P("row", "col"),
        ),
        out_specs=(P("row", "col"), P("col", "row"), P("col", "row"), P("row", "col")),
        check_vma=False,
    )
```

```python
import functools

import jax
import jax.numpy as jnp
from jax import lax
from jax.experimental import pallas as pl
from jax.experimental.pallas import tpu as pltpu
from jax.sharding import PartitionSpec as P


LAYERS = 128
F32 = jnp.float32
BF16 = jnp.bfloat16
VMEM = pl.BlockSpec(memory_space=pltpu.VMEM)
SMEM = pl.BlockSpec(memory_space=pltpu.SMEM)
ANY = pl.BlockSpec(memory_space=pl.ANY)
HBM = pl.BlockSpec(memory_space=pltpu.HBM)
LOAD_LIMIT = 44 << 20


def contract_rows(left, right):
    return lax.dot_general(left, right, (((0,), (0,)), ((), ())), preferred_element_type=F32)


def contract_cols(left, right):
    return lax.dot_general(left, right, (((1,), (1,)), ((), ())), preferred_element_type=F32)


def swap(value, axis, size, mask):
    return lax.ppermute(value, axis, [(i, i ^ mask) for i in range(size)])


def bits_of(size):
    return size.bit_length() - 1


def tiles(total, most):
    size = min(total, most)
    return [pl.ds(start, size) for start in range(0, total, size)]


def cost(flops, arrays):
    moved = sum(a.size * a.dtype.itemsize for a in arrays)
    return pl.CostEstimate(flops=flops, bytes_accessed=moved, transcendentals=0)


def into_kernel(half_ref, tokens_ref, weight_ref, own_ref, other_ref):
    width = own_ref.shape[1]
    for out_ref, half in ((other_ref, 1 - half_ref[0]), (own_ref, half_ref[0])):
        start = pl.multiple_of(half * width, width)
        out_ref[...] = jnp.dot(
            tokens_ref[...], weight_ref[:, pl.ds(start, width)], preferred_element_type=F32
        )


def halves(half_ref, tokens_ref, top_ref, bottom_ref, out_ref):
    width, middle = out_ref.shape[1], top_ref.shape[0]
    columns = pl.ds(pl.multiple_of(half_ref[0] * width, width), width)
    value = jnp.dot(tokens_ref[:, :middle], top_ref[:, columns], preferred_element_type=F32)
    value += jnp.dot(tokens_ref[:, middle:], bottom_ref[:, columns], preferred_element_type=F32)
    out_ref[...] = value


def first_kernel(half_ref, *refs):
    *block_refs, top_ref, bottom_ref, out_ref, tokens_ref = refs
    tokens_ref[...] = jnp.concatenate([ref[...] for ref in block_refs])
    halves(half_ref, tokens_ref, top_ref, bottom_ref, out_ref)


def load_kernel(starts, *refs):
    count = len(starts)
    copies = []
    for k, (start, ref, out_ref) in enumerate(zip(starts, refs, refs[count:])):
        source = ref.at[pl.ds(start, out_ref.shape[0])]
        copies.append(pltpu.make_async_copy(source, out_ref, refs[-1].at[k]))
    for copy in copies:
        copy.start()
    for copy in copies:
        copy.wait()


def load(limit, *spans):
    count = len(spans)
    shapes = tuple(jax.ShapeDtypeStruct((rows, a.shape[1]), a.dtype) for a, _, rows in spans)
    total = sum(shape.size * shape.dtype.itemsize for shape in shapes)
    return pl.pallas_call(
        functools.partial(load_kernel, [start for _, start, _ in spans]),
        out_shape=shapes,
        in_specs=[HBM] * count,
        out_specs=(VMEM,) * count,
        scratch_shapes=[pltpu.SemaphoreType.DMA((count,))],
        cost_estimate=cost(0, shapes),
        compiler_params=pltpu.CompilerParams(vmem_limit_bytes=limit),
    )(*[a for a, _, _ in spans])


def into_half(kernel, half, blocks, *weights):
    count = sum(block.shape[0] for block in blocks)
    shape = jax.ShapeDtypeStruct((count, weights[0].shape[1] // 2), F32)
    tokens = jax.ShapeDtypeStruct((count, blocks[0].shape[1]), BF16)
    shapes = (shape, tokens) if len(blocks) > 1 else (shape,)
    return pl.pallas_call(
        kernel,
        out_shape=shapes,
        in_specs=[SMEM] + [VMEM] * (len(blocks) + 2),
        out_specs=(VMEM,) * len(shapes),
        cost_estimate=cost(2 * count * weights[0].size, [*blocks, *weights, *shapes]),
        compiler_params=pltpu.CompilerParams(vmem_limit_bytes=12 << 20),
    )(half, *blocks, *weights)


def back_kernel(half_ref, tokens_ref, weight_ref, turn_ref, own_ref, other_ref, turned_ref):
    turned_ref[...] = turn_ref[...].T
    width = own_ref.shape[1]
    step = min(width, 512)
    for out_ref, half in ((other_ref, 1 - half_ref[0]), (own_ref, half_ref[0])):
        for at in range(0, width, step):
            start = pl.multiple_of(half * width + at, step)
            value = contract_cols(weight_ref[pl.ds(start, step), :], tokens_ref[...])
            out_ref[:, pl.ds(at, step)] = value.T


def into_hidden(kernel, half, tokens, weight, hidden, *turn):
    shape = jax.ShapeDtypeStruct((tokens.shape[0], hidden // 2), F32)
    turned = [jax.ShapeDtypeStruct(a.shape[::-1], a.dtype) for a in turn]
    return pl.pallas_call(
        kernel,
        out_shape=(shape, shape, *turned),
        in_specs=[SMEM, VMEM, VMEM] + [VMEM] * len(turn),
        out_specs=(VMEM, VMEM) + (VMEM,) * len(turn),
        cost_estimate=cost(2 * tokens.shape[0] * weight.size, [tokens, weight, shape, shape]),
        compiler_params=pltpu.CompilerParams(vmem_limit_bytes=12 << 20),
    )(half, tokens, weight, *turn)


def out_kernel(half_ref, gate_ref, up_ref, top_ref, bottom_ref, up_weight_ref, *rest):
    out_ref = rest[-1]
    width, middle = gate_ref.shape[1], top_ref.shape[0]
    columns = pl.ds(pl.multiple_of(half_ref[0] * width, width), width)
    for part, ref in enumerate((top_ref, bottom_ref)):
        for rows in tiles(middle, 512):
            into = pl.ds(part * middle + rows.start, rows.size)
            value = contract_cols(ref[rows, columns], gate_ref[...])
            value += contract_cols(up_weight_ref[into, columns], up_ref[...])
            if len(rest) > 1:
                out_ref[:, into] = (value + rest[0][into, :]).T
            else:
                out_ref[into, :] = value


def out_of_hidden(half, gate, up, top, bottom, up_weight, *total):
    shape = (gate.shape[0], up_weight.shape[0])
    shape = jax.ShapeDtypeStruct(shape if total else shape[::-1], F32)
    arrays = [gate, up, top, bottom, up_weight, *total]
    return pl.pallas_call(
        out_kernel,
        out_shape=shape,
        in_specs=[SMEM] + [VMEM] * len(arrays),
        out_specs=VMEM,
        cost_estimate=cost(4 * gate.size * up_weight.shape[0], arrays + [shape]),
        compiler_params=pltpu.CompilerParams(vmem_limit_bytes=21 << 20),
    )(half, *arrays)


def write_out(slices, held, sems):
    slots = held.shape[0]
    copies = []
    for step, (make, target) in enumerate(slices):
        slot = step % slots
        if step >= slots:
            copies[step - slots].wait()
        value = make().astype(held.dtype)
        held[slot] = value
        copy = pltpu.make_async_copy(held.at[slot], target, sems.at[slot])
        copy.start()
        copies.append(copy)
    for copy in copies[-slots:]:
        copy.wait()


def down_kernel(scale, half_ref, own_ref, other_ref, grads_ref, out_ref, held, sems):
    rows = held.shape[1]
    width = own_ref.shape[1]
    slices = []
    for ref, half in ((own_ref, half_ref[0]), (other_ref, 1 - half_ref[0])):
        for at in range(0, width, rows):
            make = lambda ref=ref, at=at: scale * contract_rows(ref[:, pl.ds(at, rows)], grads_ref[...])
            start = pl.multiple_of(half * width + at, rows)
            slices.append((make, out_ref.at[pl.ds(start, rows)]))
    write_out(slices, held, sems)


def down_outer(scale, half, own, other, grads):
    tokens, width = own.shape
    features = grads.shape[1]
    rows, slots = min(256, width), 4
    shape = jax.ShapeDtypeStruct((2 * width, features), BF16)
    return pl.pallas_call(
        functools.partial(down_kernel, scale),
        out_shape=shape,
        in_specs=[SMEM, VMEM, VMEM, VMEM],
        out_specs=ANY,
        scratch_shapes=[pltpu.VMEM((slots, rows, features), BF16), pltpu.SemaphoreType.DMA((slots,))],
        cost_estimate=cost(4 * tokens * width * features, [own, other, grads, shape]),
        compiler_params=pltpu.CompilerParams(vmem_limit_bytes=10 << 20),
    )(half, own, other, grads)


def up_kernel(units, count, half_ref, turned_ref, *refs):
    part_refs = refs[: len(units)]
    out_refs, held, sems = refs[-2 - count : -2], refs[-2], refs[-1]
    rows, width = held.shape[1:]
    slices = []
    for (out, own), ref in zip(units, part_refs):
        half = half_ref[0] if own else 1 - half_ref[0]
        columns = pl.ds(pl.multiple_of(half * width, width), width)
        for at in range(0, turned_ref.shape[0], rows):
            make = lambda ref=ref, at=at: jnp.dot(
                turned_ref[pl.ds(at, rows), :], ref[...], preferred_element_type=F32
            )
            slices.append((make, out_refs[out].at[pl.ds(at, rows), columns]))
    write_out(slices, held, sems)


def up_outer(half, turned, parts, begun=None, fresh=0):
    features, _ = turned.shape
    width = parts[0][2].shape[1]
    rows, slots = min(512, features), 4
    shape = jax.ShapeDtypeStruct((features, 2 * width), BF16)
    deltas = [part[2] for part in parts]
    kept = [] if begun is None else [begun]
    outs = len(kept) + fresh
    return pl.pallas_call(
        functools.partial(up_kernel, [part[:2] for part in parts], outs),
        out_shape=(shape,) * outs,
        in_specs=[SMEM] + [VMEM] * (1 + len(deltas)) + [ANY] * len(kept),
        out_specs=(ANY,) * outs,
        scratch_shapes=[pltpu.VMEM((slots, rows, width), BF16), pltpu.SemaphoreType.DMA((slots,))],
        input_output_aliases={2 + len(deltas): 0} if kept else {},
        cost_estimate=cost(2 * turned.size * width * len(deltas), [turned, *deltas, *deltas]),
        compiler_params=pltpu.CompilerParams(vmem_limit_bytes=10 << 20),
    )(half, turned, *deltas, *kept)


def gather(value, near, size, separate):
    for bit in range(3, bits_of(size)):
        value = near = jnp.concatenate([near, swap(value, "row", size, 1 << bit)])
    far = [swap(value, "row", size, 4)]
    if not separate:
        blocks = jnp.concatenate([near] + far)
        blocks = jnp.concatenate([blocks, swap(blocks, "row", size, 2)])
        return [blocks, swap(blocks, "row", size, 1)]
    far += [swap(value, "row", size, 2)]
    near_1 = swap(value, "row", size, 1)
    far += [swap(far[0], "row", size, 2)]
    near_53 = swap(jnp.concatenate(far[:2]), "row", size, 1)
    return [near, *far, near_1, near_53, swap(far[2], "row", size, 1)]


def scatter(value, size):
    def add(kept, sent, mask):
        return kept + swap(sent.astype(BF16), "row", size, mask).astype(F32)

    count = value.shape[0] // 4
    kept, last, sent_kept, sent_last = (value[k * count : (k + 1) * count] for k in range(4))
    last = add(last, sent_last, 1)
    kept = add(kept, sent_kept, 1)
    value = add(kept, last, 2)
    for bit in [2] + list(range(3, bits_of(size)))[::-1]:
        half = value.shape[0] // 2
        value = add(value[:half], value[half:], 1 << bit)
    return value


def feature_sum(parts, size):
    own, other = parts
    total = own + swap(other, "col", size, 1)
    for bit in range(1, bits_of(size)):
        sent = total.astype(BF16)
        total = total + swap(sent, "col", size, 1 << bit).astype(F32)
    return total


def per_device(sizes, inputs, out_grad, gate_weight, up_weight, down_weight):
    mult = (2.0 * LAYERS) ** (-0.5)
    rows, cols = sizes
    hidden_units = gate_weight.shape[1]
    half = (lax.axis_index("col") & 1).astype(jnp.int32).reshape(1)
    own, own_grad = load(1 << 20, (inputs, 0, inputs.shape[0]), (out_grad, 0, out_grad.shape[0]))
    blocks = gather(inputs, own, rows, True)
    grads_all = jnp.concatenate(gather(out_grad, own_grad, rows, False))
    middle = gate_weight.shape[0] // 2
    (gate_top,) = load(LOAD_LIMIT, (gate_weight, 0, middle))
    (gate_bottom,) = load(LOAD_LIMIT, (gate_weight, middle, middle))
    other, tokens_all = into_half(first_kernel, 1 - half, blocks, gate_top, gate_bottom)
    parts = [*into_half(halves, half, [tokens_all], gate_top, gate_bottom), other]
    gate = feature_sum(parts, cols)
    parts = into_hidden(into_kernel, half, tokens_all, up_weight, hidden_units)
    up = feature_sum(parts, cols)
    *parts, tokens_turned = into_hidden(back_kernel, half, grads_all, down_weight, hidden_units, tokens_all)
    back = feature_sum(parts, cols)

    hidden = (gate * jax.nn.sigmoid(gate) * up).astype(BF16)
    hidden_other = swap(hidden, "col", cols, 1)
    down_grad = down_outer(mult, half, hidden, hidden_other, grads_all)

    gate, up, back = lax.optimization_barrier((gate, up, back))
    sig = jax.nn.sigmoid(gate)
    hidden_grad = mult * back
    gate_delta = (hidden_grad * up * sig * (1.0 + gate * (1.0 - sig))).astype(BF16)
    up_delta = (hidden_grad * gate * sig).astype(BF16)
    gate_other = swap(gate_delta, "col", cols, 1)
    up_other = swap(up_delta, "col", cols, 1)

    part = out_of_hidden(half, gate_delta, up_delta, gate_top, gate_bottom, up_weight)
    part = out_of_hidden(1 - half, gate_other, up_other, gate_top, gate_bottom, up_weight, part)
    input_grad = scatter(part, rows).astype(BF16)
    (gate_grad,) = up_outer(half, tokens_turned, [(0, True, gate_delta)], fresh=1)
    parts = [(0, False, gate_other), (1, True, up_delta)]
    gate_grad, up_grad = up_outer(half, tokens_turned, parts, gate_grad, fresh=1)
    (up_grad,) = up_outer(half, tokens_turned, [(0, False, up_other)], up_grad)
    return (input_grad, gate_grad, up_grad, down_grad)


def whole(sizes, *arrays):
    return per_device(sizes, *arrays)


def solution(mesh):
    sizes = (mesh.shape["row"], mesh.shape["col"])
    return jax.shard_map(
        functools.partial(whole, sizes),
        mesh=mesh,
        in_specs=(
            P("row", "col"),
            P("row", "col"),
            P("col", "row"),
            P("col", "row"),
            P("row", "col"),
        ),
        out_specs=(P("row", "col"), P("col", "row"), P("col", "row"), P("row", "col")),
        check_vma=False,
    )
```
